32 devices in a mesh: layer: 2 (over x), gx: 4 (over z), gy: 4 (over y, core).
Axes of the slice: x: 2, y: 2, z: 4, core: 2. Of those that a mesh axis runs over, the one named last changes fastest.
Arguments:
- pressure: float32 [16, 256, 1024], P('layer', 'gx', 'gy'), may hold values from -6 to 6
- source: float32 [16, 256, 1024], P('layer', 'gx', 'gy'), may hold values from -6 to 6
- perm_x: float32 [16, 256, 1024], P('layer', 'gx', 'gy'), may hold values from 0.05 to 0.5
- perm_y: float32 [16, 256, 1024], P('layer', 'gx', 'gy'), may hold values from 0.05 to 0.5
- line_inverse: float32 [2, 8, 8, 256, 1024], P('layer', None, None, 'gx', 'gy'), may hold values from -0.98 to 1.2
- robin_below: float32 [2, 256, 1024], P('layer', 'gx', 'gy'), may hold values from -6 to 6
- tile_count: int32 [2, 16], P('layer', ('gx', 'gy')), may hold values from 1 to 48, 256 in all within a row
- perf_owner: int32 [2, 768, 1], P('layer', ('gx', 'gy')), may hold values from 0 to 15; in each aligned block of 48 rows (0 to 47, 48 to 95, ..., all dimensions but the last counted through in order) at most 3 rows name the same one
- perf_well: int32 [2, 768], P('layer', ('gx', 'gy')), may hold values from 0 to 7
- perf_column: int32 [2, 768], P('layer', ('gx', 'gy')), may hold values from 0 to 16383
- perf_index: float32 [2, 768, 8], P('layer', ('gx', 'gy')), may hold values from 0.2 to 2
- well_rate: float32 [2, 128], P('layer', ('gx', 'gy')), may hold values from -8 to 8
Outputs:
- pressure_out: float32 [16, 256, 1024], P('layer', 'gx', 'gy')
- perf_flow: float32 [2, 768, 8], P('layer', ('gx', 'gy'))
The draws below stay inside these ranges and needn't reach their ends.
Inputs may be any that keep to these rules, and one draw needn't show every extreme that they name: `tile_count`: live slots of a tile are its first ones; some tile of every group has all 48 live. `perf_owner`: among the 48 slots of one tile at most 3 name one owner.
All inputs are finite; a program needn't handle non-finite values.
Results may differ from the reference program's by a relative error of at most 0.00018.
Values sent between devices are 32-bit elements; how exact they have to be, the bound alone decides.
A program may use at most 64 MiB of HBM per device.

```python
import math
import jax
import jax.numpy as jnp
import numpy as np
from jax import lax

LZ = 8
CX = 64
CY = 256
ITERS = 2
SLOTS = 48
WO = 8
GROUPS = 2
TILES = 16
CAP = 3
NZ = 16
NX = 256
NY = 1024
N_GY = 4


def draw_line_inverse(key, part):
    keys = jax.random.split(key, 9)
    shape = (GROUPS, LZ, LZ, NX, NY)
    layer_sheet = (GROUPS, NX, NY)
    spread = jax.random.uniform(keys[0], shape, jnp.float32, -0.25, 0.25)
    diag_vals = jnp.exp(jax.random.uniform(keys[1], (GROUPS, LZ, NX, NY), jnp.float32, jnp.log(0.3), jnp.log(1.2)))
    eye_mask = (jnp.arange(LZ)[:, None] == jnp.arange(LZ)[None, :]).astype(jnp.float32)[None, :, :, None, None]
    matrix = spread * (1.0 - eye_mask) + eye_mask * diag_vals[:, :, None, :, :]
    slow_low = 0.2 ** (1.0 / max(GROUPS - 1, 1))
    slow_share = 0.5
    corners = []
    for which in range(2):
        gradual_indicator = jax.random.bernoulli(keys[2 + 3 * which], slow_share, layer_sheet)
        subset_part = jax.random.split(keys[3 + 3 * which], 3)
        gradual_amplitude = jax.random.uniform(subset_part[0], layer_sheet, jnp.float32, slow_low, 0.98)
        rapid_amplitude = jax.random.uniform(subset_part[1], layer_sheet, jnp.float32, 0.15, 0.45)
        spike_indicator = jax.random.bernoulli(subset_part[2], 0.15, layer_sheet)
        sign_flag = jax.random.bernoulli(keys[4 + 3 * which], 0.8, layer_sheet)
        amplitude_level = jnp.where(gradual_indicator, gradual_amplitude, rapid_amplitude) * jnp.where(spike_indicator, 0.5, 1.0)
        corners.append(amplitude_level * jnp.where(sign_flag, 1.0, -1.0))
    matrix = matrix.at[:, LZ - 1, 0].set(corners[0])
    matrix = matrix.at[:, 0, LZ - 1].set(corners[1])
    return matrix.astype(jnp.float32)


def plant(values, rng, smallest, top_value):
    extent = values.shape
    spot = [jax.random.randint(jax.random.fold_in(rng, axis), (), 0, extent[axis]) for axis in range(len(extent))]
    values = values.at[tuple(spot)].set(smallest)
    longest = extent.index(max(extent))
    spot[longest] = (spot[longest] + 1) % extent[longest]
    return values.at[tuple(spot)].set(top_value)


def levels(own_key, dims, shards, smallest, high):
    def one(position, blocks):
        steps = jax.random.uniform(jax.random.fold_in(jax.random.fold_in(own_key, 6), position), (blocks,), jnp.float32, smallest / len(shards), high / len(shards))
        return jnp.repeat(jnp.exp(steps), dims[position] // blocks).reshape((-1,) + (1,) * (len(dims) - position - 1))

    factor_of = one(*shards[0])
    for cut in shards[1:]:
        factor_of = factor_of * one(*cut)
    return factor_of


def length_profile(count, total, most, slope):
    portions = [(1 << 20) // math.isqrt(standing ** slope) + 1 for standing in range(2, count + 1)]
    rest, given = total - most - (count - 1), [1] * (count - 1)
    while rest > 0:
        free = [i for i in range(count - 1) if given[i] < most]
        mass, budget = sum([portions[i] for i in free]), rest
        for i in free:
            addition = min(most - given[i], max(1, budget * portions[i] // mass), rest)
            given[i] = given[i] + addition
            rest = rest - addition
    return np.array([most] + given)


def ragged_sizes(key, count, total, reach, slope):
    if count == 2:
        one = jax.random.randint(key, (), max(1, total - reach), min(reach, total - 1) + 1)
        return jnp.stack([one, total - one])
    sizes = jnp.asarray(length_profile(count, total, reach, slope), jnp.int32)
    twos = (count - 1) // 2
    giver, taker = sizes[1:1 + 2 * twos:2], sizes[2:2 + 2 * twos:2]
    room = jnp.minimum(giver - 1, reach - taker)
    moved = jax.random.randint(jax.random.fold_in(key, 1), (twos,), 0, 1 << 20) % (room + 1)
    sizes = sizes.at[1:1 + 2 * twos:2].set(giver - moved).at[2:2 + 2 * twos:2].set(taker + moved)
    return sizes[jax.random.permutation(jax.random.fold_in(key, 2), count)]


def assign_block(rng, own, number, rows, amount, top, bound, lean):
    order = jax.random.permutation(rng, amount)
    heavy_load, usual = portions_of(amount, rows * top, bound, lean, True), portions_of(amount, rows * top, bound, lean, False)
    places = jnp.arange(amount)

    def named(sizes, offset_by):
        used = int((sizes > 0).sum())
        fixed = max(1, used // 4)
        moved = fixed + (places - fixed + offset_by * (used - fixed)) % max(1, amount - fixed)
        return jnp.zeros((amount,), jnp.int32).at[order[jnp.where(places < fixed, places, moved)]].set(jnp.asarray(sizes, jnp.int32))

    sizes = jnp.where(number % 4 == 0, named(heavy_load, number // 4), named(usual, number - number // 4 - 1))
    mixed = jax.random.permutation(jax.random.fold_in(own, 3), amount)
    giver, sink = mixed[0:amount // 2 * 2:2], mixed[1:amount // 2 * 2:2]
    slack = jnp.minimum(sizes[giver] - 1, bound - sizes[sink]) // 2
    slack = jnp.where((giver == order[0]) | (sink == order[0]) | (sizes[sink] == 0), 0, jnp.maximum(slack, 0))
    moved = jax.random.randint(jax.random.fold_in(own, 4), (amount // 2,), 0, 1 << 20) % (slack + 1)
    sizes = sizes.at[giver].add(-moved).at[sink].add(moved)
    labels = jnp.searchsorted(jnp.cumsum(sizes), jnp.arange(rows * top), side="right").astype(jnp.int32)
    grid = labels.reshape(top, rows).T
    grid = grid[jax.random.permutation(jax.random.fold_in(own, 1), rows)]
    offset_by = jax.random.randint(jax.random.fold_in(own, 2), (rows, 1), 0, top)
    return jnp.take_along_axis(grid, (jnp.arange(top)[None, :] + offset_by) % top, axis=1)


def portions_of(count, total, most, skew, full):
    loads = [(1 << 20) // math.isqrt(standing ** skew) + 1 for standing in range(1, count + 1)]
    largest = most if full else min(most, max(-(-total // count), total * loads[0] // sum(loads)))
    least = 1 if total - largest >= count - 1 else 0
    given, spare = [largest] + [least] * (count - 1), total - largest - least * (count - 1)
    while spare > 0:
        movable = [i for i in range(1, count) if given[i] < largest] or [i for i in range(1, count) if given[i] < most]
        pool, remaining = sum([loads[i] for i in movable]), spare
        for i in movable:
            addition = min(most - given[i], max(1, remaining * loads[i] // pool), spare)
            given[i] = given[i] + addition
            spare = spare - addition
    return np.array(given)


def centred(stream_key, shape, width, limit, shards=(), kind=jnp.bfloat16):
    entries = width * jax.random.normal(stream_key, shape, jnp.float32)
    if shards:
        entries = entries * levels(stream_key, shape, shards, -0.22, 0.18)
    return jnp.clip(entries, -limit, limit).astype(kind)


def setup_inputs(seed: int = 0) -> dict:
    key_list = jax.random.split(jax.random.key(seed), 13)
    pressure = centred(key_list[0], (NZ, NX, NY), 1.0, 6.0, ((0, 2), (1, 4), (2, 4)), jnp.float32)
    source = centred(key_list[1], (NZ, NX, NY), 1.0, 6.0, ((0, 2), (1, 4), (2, 4)), jnp.float32)
    perm_x = jnp.clip(jnp.exp(math.log(0.5) - 2.3025851 * jax.random.uniform(key_list[2], (NZ, NX, NY), jnp.float32) ** levels(key_list[2], (NZ, NX, NY), ((0, 2), (1, 4), (2, 4)), -0.2, 0.2)), 0.05, 0.5)
    perm_y = jnp.clip(jnp.exp(math.log(0.5) - 2.3025851 * jax.random.uniform(key_list[3], (NZ, NX, NY), jnp.float32) ** levels(key_list[3], (NZ, NX, NY), ((0, 2), (1, 4), (2, 4)), -0.2, 0.2)), 0.05, 0.5)
    line_inverse = draw_line_inverse(jax.random.fold_in(key_list[12], 71), 0)
    robin_below = centred(key_list[5], (GROUPS, NX, NY), 1.0, 6.0, ((0, 2), (1, 4), (2, 4)), jnp.float32)
    tile_count = jax.vmap(lambda own: ragged_sizes(own, TILES, TILES * SLOTS // 3, SLOTS, 2))(jax.random.split(key_list[6], GROUPS)).reshape((GROUPS, TILES)).astype(jnp.int32)
    perf_owner_keys = jax.random.split(jax.random.fold_in(key_list[7], 1), GROUPS * (TILES * SLOTS) // SLOTS)
    perf_owner_turns = jax.random.permutation(jax.random.fold_in(key_list[7], 3), GROUPS * (TILES * SLOTS) // SLOTS)
    perf_owner = jax.vmap(lambda own, number: assign_block(jax.random.fold_in(key_list[7], 2), own, number, SLOTS, TILES, 1, CAP, 2))(perf_owner_keys, perf_owner_turns).reshape((GROUPS, TILES * SLOTS, 1))
    perf_well = plant(jax.random.randint(key_list[8], (GROUPS, TILES * SLOTS), 0, WO), jax.random.fold_in(key_list[8], 1), 0, WO - 1).astype(jnp.int32)
    perf_column = plant(jax.random.randint(key_list[9], (GROUPS, TILES * SLOTS), 0, CX * CY), jax.random.fold_in(key_list[9], 1), 0, (CX * CY) - 1).astype(jnp.int32)
    perf_index = jnp.clip(jnp.exp(math.log(2.0) - 2.3025851 * jax.random.uniform(key_list[10], (GROUPS, TILES * SLOTS, LZ), jnp.float32) ** levels(key_list[10], (GROUPS, TILES * SLOTS, LZ), ((0, 2), (1, 16)), -0.2, 0.2)), 0.2, 2.0)
    well_rate = centred(key_list[11], (GROUPS, TILES * WO), 2.0, 8.0, ((0, 2), (1, 16)), jnp.float32)
    return {"pressure": pressure, "source": source, "perm_x": perm_x, "perm_y": perm_y, "line_inverse": line_inverse, "robin_below": robin_below, "tile_count": tile_count, "perf_owner": perf_owner, "perf_well": perf_well, "perf_column": perf_column, "perf_index": perf_index, "well_rate": well_rate}


HIGHEST_PRECISION = lax.Precision.HIGHEST


def neighbours(padded_field, rock_x, rock_y, perm_x, perm_y):
    east_term = 0.5 * (perm_x + rock_x[:, 2:, 1:-1]) * padded_field[:, 2:, 1:-1]
    west_term = 0.5 * (perm_x + rock_x[:, :-2, 1:-1]) * padded_field[:, :-2, 1:-1]
    north_term = 0.5 * (perm_y + rock_y[:, 1:-1, 2:]) * padded_field[:, 1:-1, 2:]
    south_term = 0.5 * (perm_y + rock_y[:, 1:-1, :-2]) * padded_field[:, 1:-1, :-2]
    return (east_term + west_term) + (north_term + south_term)


def reference(pressure, source, perm_x, perm_y, line_inverse, robin_below, tile_count, perf_owner, perf_well, perf_column, perf_index, well_rate):
    group_total = GROUPS
    tile_total = TILES
    border = ((0, 0), (1, 1), (1, 1))
    rock_x = jnp.pad(perm_x, border)
    rock_y = jnp.pad(perm_y, border)
    live_slot = (jnp.arange(SLOTS).astype(jnp.int32)[None, None, :] < tile_count[:, :, None]).astype(jnp.float32)[..., None]
    tile_ids = jnp.arange(tile_total).astype(jnp.int32)
    column = perf_column.reshape(group_total, tile_total, SLOTS)
    cell_x = (tile_ids // N_GY)[None, :, None] * CX + column // CY
    cell_y = (tile_ids % N_GY)[None, :, None] * CY + column % CY
    full_shape = (group_total, tile_total, SLOTS, LZ)
    layer_ids = jnp.broadcast_to((jnp.arange(group_total)[:, None, None, None] * LZ + jnp.arange(LZ)[None, None, None, :]).astype(jnp.int32), full_shape)
    cell_x4 = jnp.broadcast_to(cell_x[..., None], full_shape)
    cell_y4 = jnp.broadcast_to(cell_y[..., None], full_shape)
    index_rows = perf_index.reshape(full_shape)
    well_ids = perf_owner.reshape(group_total, tile_total, SLOTS) * WO + perf_well.reshape(group_total, tile_total, SLOTS)
    group_ids = jnp.broadcast_to(jnp.arange(group_total).astype(jnp.int32)[:, None, None], well_ids.shape)
    field_now = pressure
    lower_data = robin_below
    slot_flow = jnp.zeros(full_shape, jnp.float32)
    for sweep_step in range(ITERS):
        lateral = neighbours(jnp.pad(field_now, border), rock_x, rock_y, perm_x, perm_y)
        at_slots = field_now[layer_ids, cell_x4, cell_y4]
        index_sum = jnp.zeros((group_total, tile_total * WO), jnp.float32).at[group_ids, well_ids].add(jnp.sum(index_rows * live_slot, axis=-1))
        weighted_sum = jnp.zeros((group_total, tile_total * WO), jnp.float32).at[group_ids, well_ids].add(jnp.sum(index_rows * at_slots * live_slot, axis=-1))
        bottom_hole = (well_rate + weighted_sum) / (index_sum + 1.0)
        slot_flow = index_rows * (bottom_hole[group_ids, well_ids][..., None] - at_slots) * live_slot
        well_term = jnp.zeros_like(field_now).at[layer_ids, cell_x4, cell_y4].add(slot_flow)
        rhs = (source + lateral) + well_term
        blocks = rhs.reshape(group_total, LZ, NX, NY)
        solved = jnp.einsum('gijxy,gjxy->gixy', line_inverse, blocks, precision=HIGHEST_PRECISION)
        upper_trace = jnp.zeros((NX, NY), jnp.float32)
        upper_list = [upper_trace]
        for group_id in range(group_total - 1):
            carried = (solved[group_id, LZ - 1] + line_inverse[group_id, LZ - 1, LZ - 1] * lower_data[group_id]) - lower_data[group_id]
            upper_trace = line_inverse[group_id, LZ - 1, 0] * upper_trace + carried
            upper_list.append(upper_trace)
        upper_all = jnp.stack(upper_list)
        lower_trace = jnp.zeros((NX, NY), jnp.float32)
        lower_list = [lower_trace for group_id in range(group_total)]
        for group_id in range(group_total - 1, 0, -1):
            carried = (solved[group_id, 0] + line_inverse[group_id, 0, 0] * upper_all[group_id]) - upper_all[group_id]
            lower_trace = line_inverse[group_id, 0, LZ - 1] * lower_trace + carried
            lower_list[group_id - 1] = lower_trace
        lower_data = jnp.stack(lower_list)
        updated = solved + line_inverse[:, :, 0] * upper_all[:, None] + line_inverse[:, :, LZ - 1] * lower_data[:, None]
        field_now = updated.reshape(NZ, NX, NY)
    return field_now, slot_flow.reshape(group_total, tile_total * SLOTS, LZ)
```

```python
import functools

import jax
import jax.numpy as jnp
from jax import lax
from jax.experimental import pallas as pl
from jax.experimental.pallas import tpu as pltpu
from jax.sharding import PartitionSpec as P

ITERS = 2
MESH = pl.DeviceIdType.MESH
F32 = jnp.float32
BF16 = jnp.bfloat16
ROWS = 8


def pieces(value):
    high = value.astype(BF16)
    rest = value - high.astype(F32)
    middle = rest.astype(BF16)
    low = (rest - middle.astype(F32)).astype(BF16)
    return jnp.concatenate([high, middle, low], axis=0)


def as_column(row):
    n = row.shape[1]
    eye = lax.broadcasted_iota(jnp.int32, (n, n), 0) == lax.broadcasted_iota(jnp.int32, (n, n), 1)
    return jnp.sum(jnp.where(eye, jnp.broadcast_to(row, (n, n)), 0.0), axis=1, keepdims=True)


def kernel(
    dims,
    pressure,
    source,
    perm_x,
    perm_y,
    inverse,
    robin,
    count_in,
    owner_in,
    well_in,
    column_in,
    index_in,
    rate_in,
    field_out,
    flow_out,
    field,
    src,
    kx,
    ky,
    inv,
    lower,
    count_v,
    owner_v,
    well_v,
    column_v,
    index_v,
    rate_v,
    upper,
    rhs,
    solved,
    flow_v,
    halo_mult_x,
    halo_mult_y,
    well_send0,
    well_recv0,
    well_send1,
    well_recv1,
    row_send,
    row_recv,
    col_send,
    col_recv,
    coef_recv,
    down_send,
    down_recv,
    up_send,
    up_recv,
    load_sem,
    store_sem,
    well_ssem,
    well_rsem,
    halo_ssem,
    halo_rsem,
    coef_ssem,
    coef_rsem,
    down_ssem,
    down_rsem,
    up_ssem,
    up_rsem,
):
    groups, n_gx, n_gy = dims
    tiles = n_gx * n_gy
    depth, width_x, width_y = field.shape
    slots = well_v.shape[1]
    own_wells = rate_v.shape[1]
    wells = tiles * own_wells
    me_l, me_x, me_y = lax.axis_index("layer"), lax.axis_index("gx"), lax.axis_index("gy")
    me = me_x * n_gy + me_y

    loads = [
        pltpu.make_async_copy(a, b, load_sem.at[i])
        for i, (a, b) in enumerate(
            [
                (pressure, field),
                (column_in, column_v),
                (well_in, well_v),
                (owner_in, owner_v),
                (index_in, index_v),
                (count_in, count_v),
                (rate_in, rate_v),
                (perm_x, kx),
                (perm_y, ky),
                (source, src),
                (robin, lower),
                (inverse, inv),
            ]
        )
    ]
    for load in loads:
        load.start()

    def peer(step):
        other = lax.rem(me + step, tiles)
        return {"gx": lax.div(other, n_gy), "gy": lax.rem(other, n_gy)}

    barrier = pltpu.get_barrier_semaphore()
    for step in range(1, tiles):
        pl.semaphore_signal(barrier, inc=1, device_id=peer(step), device_id_type=MESH)
    for step in range(1, groups):
        pl.semaphore_signal(
            barrier, inc=1, device_id={"layer": lax.rem(me_l + step, groups)}, device_id_type=MESH
        )

    for load in loads[1:7]:
        load.wait()
    live = lax.broadcasted_iota(jnp.int32, (slots, 1), 0) < count_v[...]
    column_row = column_v[...]
    column_col = as_column(column_row.astype(F32)).astype(jnp.int32)
    lane_x = lax.broadcasted_iota(jnp.int32, (slots, width_x), 1)
    in_x = (column_col >= lane_x * width_y) & (column_col < lane_x * width_y + width_y)
    x_of = jnp.sum(jnp.where(in_x, lane_x.astype(F32), 0.0), axis=1, keepdims=True).astype(jnp.int32)
    in_y = lax.broadcasted_iota(jnp.int32, (slots, width_y), 1) == column_col - x_of * width_y
    hot_x = jnp.where(in_x, 1.0, 0.0).astype(BF16)
    hot_x3 = jnp.concatenate([hot_x] * 3, axis=1)
    row_x = lax.broadcasted_iota(jnp.int32, (width_x, slots), 0)
    hot_xt = jnp.where(
        (column_row >= row_x * width_y) & (column_row < row_x * width_y + width_y), 1.0, 0.0
    ).astype(BF16)
    hot_xt3 = jnp.concatenate([hot_xt] * 3, axis=1)
    well_col = as_column(well_v[...].astype(F32)).astype(jnp.int32)
    well_id = owner_v[0] * own_wells + well_col
    member = jnp.where(
        (lax.broadcasted_iota(jnp.int32, (slots, wells), 1) == well_id) & live, 1.0, 0.0
    )
    index = index_v[...]
    rate_col = as_column(rate_v[...])
    rate_spot = (
        lax.broadcasted_iota(jnp.int32, (own_wells, wells), 1)
        == lax.broadcasted_iota(jnp.int32, (own_wells, wells), 0) + me * own_wells
    )
    rate_row = jnp.sum(jnp.where(rate_spot, rate_col, 0.0), axis=0, keepdims=True)
    layer_lane = lax.broadcasted_iota(jnp.int32, (slots, depth), 1)

    def gathered():
        at = jnp.zeros((slots, depth), F32)
        for l in range(depth):
            picked = jnp.dot(hot_x3, pieces(field[l]), preferred_element_type=F32)
            one = jnp.sum(jnp.where(in_y, picked, 0.0), axis=1, keepdims=True)
            at = jnp.where(layer_lane == l, one, at)
        return at

    def well_row(at):
        share = jnp.sum(index * at, axis=1, keepdims=True)
        return jnp.sum(share * member, axis=0, keepdims=True) + rate_row

    def well_copy(it, step):
        send, recv = ((well_send0, well_recv0), (well_send1, well_recv1))[it]
        return pltpu.make_async_remote_copy(
            src_ref=send,
            dst_ref=recv.at[step],
            send_sem=well_ssem.at[it, step],
            recv_sem=well_rsem.at[it, step],
            device_id=peer(step),
            device_id_type=MESH,
        )

    sides = (
        ("gx", me_x, -1, me_x > 0),
        ("gx", me_x, 1, me_x < n_gx - 1),
        ("gy", me_y, -1, me_y > 0),
        ("gy", me_y, 1, me_y < n_gy - 1),
    )

    def halo_copy(it, side):
        axis, mine, way, _ = sides[side]
        send, recv = (row_send, row_recv) if side < 2 else (col_send, col_recv)
        width = slice(0, 2 if it == 0 else 1)
        if side < 2:
            source_ref = send.at[it, side, width]
            target_ref = recv.at[it, 1 - side, width]
        else:
            source_ref = send.at[it, side - 2]
            target_ref = recv.at[it, 3 - side]
        return pltpu.make_async_remote_copy(
            src_ref=source_ref,
            dst_ref=target_ref,
            send_sem=halo_ssem.at[it, side],
            recv_sem=halo_rsem.at[it, side ^ 1],
            device_id={axis: mine + way},
            device_id_type=MESH,
        )

    def halo_landing(it, side):
        axis, mine, way, _ = sides[side]
        if side < 2:
            width = slice(0, 2 if it == 0 else 1)
            ref, other = row_recv.at[it, side, width], row_send.at[it, 1 - side, width]
        else:
            ref, other = col_recv.at[it, side - 2], col_send.at[it, 3 - side]
        return pltpu.make_async_remote_copy(
            src_ref=other,
            dst_ref=ref,
            send_sem=halo_ssem.at[it, side],
            recv_sem=halo_rsem.at[it, side],
            device_id={axis: mine + way},
            device_id_type=MESH,
        )

    lane128 = lax.broadcasted_iota(jnp.int32, (width_x, 128), 1)

    def packed_columns(arrays, lane):
        out = jnp.zeros((width_x, 128), F32)
        at = 0
        for ref in arrays:
            for l in range(depth):
                out = jnp.where(lane128 == at, ref[l, :, lane : lane + 1], out)
                at += 1
        return out

    def stage_halos(it):
        for l in range(depth):
            row_send[it, 0, 0, l : l + 1, :] = field[l, 0:1, :]
            row_send[it, 1, 0, l : l + 1, :] = field[l, width_x - 1 : width_x, :]
            if it == 0:
                row_send[it, 0, 1, l : l + 1, :] = kx[l, 0:1, :]
                row_send[it, 1, 1, l : l + 1, :] = kx[l, width_x - 1 : width_x, :]
        arrays = (field, ky) if it == 0 else (field,)
        col_send[it, 0] = packed_columns(arrays, 0)
        col_send[it, 1] = packed_columns(arrays, width_y - 1)
        for side in range(4):

            @pl.when(jnp.logical_not(sides[side][3]))
            def _():
                if side < 2:
                    row_recv[it, side] = jnp.zeros(row_recv.shape[2:], F32)
                else:
                    col_recv[it, side - 2] = jnp.zeros(col_recv.shape[2:], F32)

    def start_halos(it):
        for side in range(4):
            @pl.when(sides[side][3])
            def _():
                halo_copy(it, side).start()

    def wait_halos(it):
        for side in range(4):
            @pl.when(sides[side][3])
            def _():
                halo_landing(it, side).wait_recv()

    last_x = lax.broadcasted_iota(jnp.int32, (width_x, width_y), 0) == width_x - 1
    first_x = lax.broadcasted_iota(jnp.int32, (width_x, width_y), 0) == 0
    last_y = lax.broadcasted_iota(jnp.int32, (width_x, width_y), 1) == width_y - 1
    first_y = lax.broadcasted_iota(jnp.int32, (width_x, width_y), 1) == 0

    def next_x(value, row):
        return jnp.where(last_x, row, pltpu.roll(value, width_x - 1, 0))

    def next_y(value, col):
        return jnp.where(last_y, col, pltpu.roll(value, width_y - 1, 1))

    def face_coefficients():
        for l in range(depth):
            row = kx[l, 0:1, :]
            halo_mult_x[l : l + 1, :] = 0.5 * (row + row_recv[0, 0, 1, l : l + 1, :])
            mult = kx[l]
            kx[l] = 0.5 * (mult + next_x(mult, row_recv[0, 1, 1, l : l + 1, :]))
            mult = ky[l]
            ky[l] = 0.5 * (mult + next_y(mult, col_recv[0, 1, :, depth + l : depth + l + 1]))
        halo_mult_y[...] = 0.5 * (col_send[0, 0] + col_recv[0, 0])

    def lateral_sum(it):
        for l in range(depth):
            now = field[l]
            face_x, face_y = kx[l], ky[l]
            east = face_x * next_x(now, row_recv[it, 1, 0, l : l + 1, :])
            west_row = halo_mult_x[l : l + 1, :] * row_recv[it, 0, 0, l : l + 1, :]
            west = jnp.where(first_x, west_row, pltpu.roll(face_x * now, 1, 0))
            north = face_y * next_y(now, col_recv[it, 1, :, l : l + 1])
            south_col = halo_mult_y[:, depth + l : depth + l + 1] * col_recv[it, 0, :, l : l + 1]
            south = jnp.where(first_y, south_col, pltpu.roll(face_y * now, 1, 1))
            rhs[l] = src[l] + ((east + west) + (north + south))

    def layer_copy(ref, target, ssem, rsem, other):
        return pltpu.make_async_remote_copy(
            src_ref=ref,
            dst_ref=target,
            send_sem=ssem,
            recv_sem=rsem,
            device_id={"layer": other},
            device_id_type=MESH,
        )

    last = depth - 1
    coef_at = ((0, 0), (0, last), (last, 0))[: 1 if groups == 2 else 3]

    def coef_copy(which, sender, other):
        i, j = coef_at[which]
        return layer_copy(
            inv.at[i, j],
            coef_recv.at[sender, which],
            coef_ssem.at[other, which],
            coef_rsem.at[sender, which],
            other,
        )

    def coef_sent(which, sender, other):
        if which == 0:
            return other < sender
        if which == 1:
            return other < sender < groups - 1
        return 0 < sender < groups - 1

    def down_copy(it, sender, other):
        return layer_copy(
            down_send.at[it], down_recv.at[it, sender], down_ssem.at[it, other],
            down_rsem.at[it, sender], other,
        )

    def up_copy(it, sender, other):
        return layer_copy(
            up_send.at[it], up_recv.at[it, sender], up_ssem.at[it, other],
            up_rsem.at[it, sender], other,
        )

    def layer_sends(act, which):
        for g in range(groups):

            @pl.when(me_l == g)
            def _():
                for other in range(groups):
                    if other == g:
                        continue
                    if which == "coef":
                        for c in range(len(coef_at)):
                            if coef_sent(c, g, other):
                                getattr(coef_copy(c, g, other), act)()
                    else:
                        it = which
                        if g < groups - 1:
                            getattr(down_copy(it, g, other), act)()
                        if other < g:
                            getattr(up_copy(it, g, other), act)()

    def chunk_loop(body):
        def step(c, carry):
            body(pl.ds(pl.multiple_of(c * ROWS, ROWS), ROWS))
            return carry

        lax.fori_loop(0, width_x // ROWS, step, 0)

    def dot_layer(i, rows, terms):
        total = inv[i, 0, rows, :] * terms[0]
        for j in range(1, depth):
            total = total + inv[i, j, rows, :] * terms[j]
        return total

    def solve_faces(it):
        def body(rows):
            terms = [rhs[j, rows, :] for j in range(depth)]
            bottom = dot_layer(last, rows, terms)
            top = dot_layer(0, rows, terms)
            solved[last, rows, :] = bottom
            solved[0, rows, :] = top
            below = lower[rows, :]
            nothing = jnp.zeros_like(below)
            down_send[it, rows, :] = inv[last, 0, rows, :] * nothing + (
                (bottom + inv[last, last, rows, :] * below) - below
            )
            up_send[it, rows, :] = inv[0, last, rows, :] * nothing + top

        chunk_loop(body)

    def solve_rest():
        def body(rows):
            terms = [rhs[j, rows, :] for j in range(depth)]
            for i in range(1, depth - 1):
                solved[i, rows, :] = dot_layer(i, rows, terms)

        chunk_loop(body)

    def sweeps(it):
        for g in range(groups):

            @pl.when(me_l == g)
            def _():
                for k in range(groups):
                    if k == g:
                        continue
                    if k < groups - 1:
                        down_copy(it, k, k).wait_recv()
                    if k > g:
                        up_copy(it, k, k).wait_recv()
                    if it == 0:
                        for c in range(len(coef_at)):
                            if coef_sent(c, k, g):
                                coef_copy(c, k, k).wait_recv()

                def body(rows):
                    def coef(which, k):
                        i, j = coef_at[which]
                        return inv[i, j, rows, :] if k == g else coef_recv[k, which, rows, :]

                    above = [jnp.zeros((ROWS, width_y), F32)]
                    for k in range(groups - 1):
                        value = down_send[it, rows, :] if k == g else down_recv[it, k, rows, :]
                        if k > 0:
                            value = coef(2, k) * above[k] + value
                        above.append(value)
                    below = jnp.zeros((ROWS, width_y), F32)
                    for k in range(groups - 1, g, -1):
                        value = (up_recv[it, k, rows, :] + coef(0, k) * above[k]) - above[k]
                        if k < groups - 1:
                            value = coef(1, k) * below + value
                        below = value
                    upper[rows, :] = above[g]
                    lower[rows, :] = below

                chunk_loop(body)

    def update():
        def body(rows):
            above, below = upper[rows, :], lower[rows, :]
            for i in range(depth):
                field[i, rows, :] = (
                    solved[i, rows, :]
                    + inv[i, 0, rows, :] * above
                    + inv[i, last, rows, :] * below
                )

        chunk_loop(body)

    index_total = None
    for it in range(ITERS):
        if it == 0:
            loads[0].wait()
        at = gathered()
        if it == 0:
            index_row = jnp.sum(
                jnp.sum(index, axis=1, keepdims=True) * member, axis=0, keepdims=True
            )
            well_send0[...] = jnp.concatenate([well_row(at), index_row], axis=1)
            pl.semaphore_wait(barrier, tiles - 1 + groups - 1)
        else:
            well_send1[...] = well_row(at)
        for step in range(1, tiles):
            well_copy(it, step).start()
        if it == 0:
            loads[7].wait()
            loads[8].wait()
        stage_halos(it)
        start_halos(it)
        if it == 0:
            for load in loads[9:]:
                load.wait()
            layer_sends("start", "coef")
        wait_halos(it)
        if it == 0:
            face_coefficients()
        lateral_sum(it)
        total = (well_send0, well_send1)[it][...]
        for step in range(1, tiles):
            well_copy(it, step).wait_recv()
        for step in range(1, tiles):
            total = total + (well_recv0, well_recv1)[it][step]
        if it == 0:
            index_total = total[:, wells:] + 1.0
            total = total[:, :wells]
        bottom_hole = total / index_total
        hole = jnp.sum(member * bottom_hole, axis=1, keepdims=True)
        flow = jnp.where(live, index * (hole - at), 0.0)
        if it == ITERS - 1:
            flow_v[...] = flow
            flow_store = pltpu.make_async_copy(flow_v, flow_out, store_sem.at[0])
            flow_store.start()
        for l in range(depth):
            spread = jnp.where(in_y, flow[:, l : l + 1], 0.0)
            rhs[l] = rhs[l] + jnp.dot(hot_xt3, pieces(spread), preferred_element_type=F32)
        solve_faces(it)
        layer_sends("start", it)
        solve_rest()
        sweeps(it)
        update()
    field_store = pltpu.make_async_copy(field, field_out, store_sem.at[1])
    field_store.start()
    for it in range(ITERS):
        for step in range(1, tiles):
            well_copy(it, step).wait_send()
        for side in range(4):

            @pl.when(sides[side][3])
            def _():
                halo_copy(it, side).wait_send()

        layer_sends("wait_send", it)
    layer_sends("wait_send", "coef")
    flow_store.wait()
    field_store.wait()


def shards(
    pressure,
    source,
    perm_x,
    perm_y,
    line_inverse,
    robin_below,
    tile_count,
    perf_owner,
    perf_well,
    perf_column,
    perf_index,
    well_rate,
):
    depth, width_x, width_y = pressure.shape
    groups, n_gx, n_gy = (lax.axis_size(a) for a in ("layer", "gx", "gy"))
    tiles = n_gx * n_gy
    slots = perf_well.shape[1]
    own_wells = well_rate.shape[1]
    wells = tiles * own_wells
    sheet = (width_x, width_y)
    coefs = 1 if groups == 2 else 3
    anywhere = pl.BlockSpec(memory_space=pl.ANY)
    dma = pltpu.SemaphoreType.DMA
    i32 = jnp.int32
    call = pl.pallas_call(
        functools.partial(kernel, (groups, n_gx, n_gy)),
        out_shape=(
            jax.ShapeDtypeStruct(pressure.shape, F32),
            jax.ShapeDtypeStruct((slots, depth), F32),
        ),
        in_specs=[anywhere] * 12,
        out_specs=(anywhere, anywhere),
        scratch_shapes=[
            pltpu.VMEM(pressure.shape, F32),
            pltpu.VMEM(pressure.shape, F32),
            pltpu.VMEM(pressure.shape, F32),
            pltpu.VMEM(pressure.shape, F32),
            pltpu.VMEM((depth, depth) + sheet, F32),
            pltpu.VMEM(sheet, F32),
            pltpu.VMEM((1, 1), i32),
            pltpu.VMEM((1, slots, 1), i32),
            pltpu.VMEM((1, slots), i32),
            pltpu.VMEM((1, slots), i32),
            pltpu.VMEM((slots, depth), F32),
            pltpu.VMEM((1, own_wells), F32),
            pltpu.VMEM(sheet, F32),
            pltpu.VMEM(pressure.shape, F32),
            pltpu.VMEM(pressure.shape, F32),
            pltpu.VMEM((slots, depth), F32),
            pltpu.VMEM((depth, width_y), F32),
            pltpu.VMEM((width_x, 128), F32),
            pltpu.VMEM((1, 2 * wells), F32),
            pltpu.VMEM((tiles, 1, 2 * wells), F32),
            pltpu.VMEM((1, wells), F32),
            pltpu.VMEM((tiles, 1, wells), F32),
            pltpu.VMEM((ITERS, 2, 2, depth, width_y), F32),
            pltpu.VMEM((ITERS, 2, 2, depth, width_y), F32),
            pltpu.VMEM((ITERS, 2, width_x, 128), F32),
            pltpu.VMEM((ITERS, 2, width_x, 128), F32),
            pltpu.VMEM((groups, coefs) + sheet, F32),
            pltpu.VMEM((ITERS,) + sheet, F32),
            pltpu.VMEM((ITERS, groups) + sheet, F32),
            pltpu.VMEM((ITERS,) + sheet, F32),
            pltpu.VMEM((ITERS, groups) + sheet, F32),
            dma((12,)),
            dma((2,)),
            dma((ITERS, tiles)),
            dma((ITERS, tiles)),
            dma((ITERS, 4)),
            dma((ITERS, 4)),
            dma((groups, coefs)),
            dma((groups, coefs)),
            dma((ITERS, groups)),
            dma((ITERS, groups)),
            dma((ITERS, groups)),
            dma((ITERS, groups)),
        ],
        compiler_params=pltpu.CompilerParams(collective_id=0, has_side_effects=True),
        name="window",
    )
    field, flow = call(
        pressure,
        source,
        perm_x,
        perm_y,
        line_inverse[0],
        robin_below[0],
        tile_count,
        perf_owner,
        perf_well,
        perf_column,
        perf_index[0],
        well_rate,
    )
    return field, flow[None]


def solution(mesh):
    placed = (
        P("layer", "gx", "gy"),
        P("layer", "gx", "gy"),
        P("layer", "gx", "gy"),
        P("layer", "gx", "gy"),
        P("layer", None, None, "gx", "gy"),
        P("layer", "gx", "gy"),
        P("layer", ("gx", "gy")),
        P("layer", ("gx", "gy"), None),
        P("layer", ("gx", "gy")),
        P("layer", ("gx", "gy")),
        P("layer", ("gx", "gy"), None),
        P("layer", ("gx", "gy")),
    )
    return jax.shard_map(
        shards,
        mesh=mesh,
        in_specs=placed,
        out_specs=(P("layer", "gx", "gy"), P("layer", ("gx", "gy"), None)),
        check_vma=False,
    )
```

```python
import functools

import jax
import jax.numpy as jnp
from jax import lax
from jax.experimental import pallas as pl
from jax.experimental.pallas import tpu as pltpu
from jax.sharding import PartitionSpec as P

ITERS = 2
LIMIT = 24 << 20
MESH = pl.DeviceIdType.MESH
F32 = jnp.float32
BF16 = jnp.bfloat16
ROWS = 8


def pieces(value):
    high = value.astype(BF16)
    rest = value - high.astype(F32)
    middle = rest.astype(BF16)
    low = (rest - middle.astype(F32)).astype(BF16)
    return jnp.concatenate([high, middle, low], axis=0)


def as_column(row):
    n = row.shape[1]
    eye = lax.broadcasted_iota(jnp.int32, (n, n), 0) == lax.broadcasted_iota(jnp.int32, (n, n), 1)
    return jnp.sum(jnp.where(eye, jnp.broadcast_to(row, (n, n)), 0.0), axis=1, keepdims=True)


def as_row(column):
    n = column.shape[0]
    eye = lax.broadcasted_iota(jnp.int32, (n, n), 0) == lax.broadcasted_iota(jnp.int32, (n, n), 1)
    return jnp.sum(jnp.where(eye, jnp.broadcast_to(column, (n, n)), 0.0), axis=0, keepdims=True)


def keep(field_in, flow_in, field_out, flow_out, sem):
    copies = [
        pltpu.make_async_copy(field_in, field_out, sem.at[0]),
        pltpu.make_async_copy(flow_in, flow_out, sem.at[1]),
    ]
    for copy in copies:
        copy.start()
    for copy in copies:
        copy.wait()


def kernel(
    dims,
    pressure,
    source,
    perm_x,
    perm_y,
    inverse,
    robin,
    count_in,
    owner_in,
    well_in,
    column_in,
    index_in,
    rate_in,
    field_out,
    flow_out,
    field,
    src,
    kx,
    ky,
    inv,
    lower,
    count_v,
    owner_v,
    well_v,
    column_v,
    index_v,
    rate_v,
    upper,
    rhs,
    solved,
    flow_v,
    halo_mult_x,
    halo_mult_y,
    well_send0,
    well_recv0,
    well_send1,
    well_recv1,
    row_send,
    row_recv,
    col_send,
    col_recv,
    coef_recv,
    down_send,
    down_recv,
    up_send,
    up_recv,
    load_sem,
    store_sem,
    well_ssem,
    well_rsem,
    halo_ssem,
    halo_rsem,
    coef_ssem,
    coef_rsem,
    down_ssem,
    down_rsem,
    up_ssem,
    up_rsem,
):
    groups, n_gx, n_gy = dims
    tiles = n_gx * n_gy
    depth, width_x, width_y = field.shape
    slots = well_v.shape[1]
    own_wells = rate_v.shape[1]
    wells = tiles * own_wells
    me_l, me_x, me_y = lax.axis_index("layer"), lax.axis_index("gx"), lax.axis_index("gy")
    me = me_x * n_gy + me_y

    loads = [
        pltpu.make_async_copy(a, b, load_sem.at[i])
        for i, (a, b) in enumerate(
            [
                (pressure, field),
                (column_in, column_v),
                (well_in, well_v),
                (owner_in, owner_v),
                (index_in, index_v),
                (count_in, count_v),
                (rate_in, rate_v),
                (perm_x, kx),
                (perm_y, ky),
                (source, src),
                (robin, lower),
                (inverse, inv),
            ]
        )
    ]
    for load in loads:
        load.start()

    def peer(step):
        other = lax.rem(me + step, tiles)
        return {"gx": lax.div(other, n_gy), "gy": lax.rem(other, n_gy)}

    barrier = pltpu.get_barrier_semaphore()
    for step in range(1, tiles):
        pl.semaphore_signal(barrier, inc=1, device_id=peer(step), device_id_type=MESH)
    for step in range(1, groups):
        pl.semaphore_signal(
            barrier, inc=1, device_id={"layer": lax.rem(me_l + step, groups)}, device_id_type=MESH
        )

    for load in loads[1:7]:
        load.wait()
    live = lax.broadcasted_iota(jnp.int32, (slots, 1), 0) < count_v[...]
    column_row = column_v[...]
    column_col = as_column(column_row.astype(F32)).astype(jnp.int32)
    lane_x = lax.broadcasted_iota(jnp.int32, (slots, width_x), 1)
    in_x = (column_col >= lane_x * width_y) & (column_col < lane_x * width_y + width_y)
    x_of = jnp.sum(jnp.where(in_x, lane_x.astype(F32), 0.0), axis=1, keepdims=True).astype(jnp.int32)
    in_y = lax.broadcasted_iota(jnp.int32, (slots, width_y), 1) == column_col - x_of * width_y
    hot_x = jnp.where(in_x, 1.0, 0.0).astype(BF16)
    hot_x3 = jnp.concatenate([hot_x] * 3, axis=1)
    row_x = lax.broadcasted_iota(jnp.int32, (width_x, slots), 0)
    hot_xt = jnp.where(
        (column_row >= row_x * width_y) & (column_row < row_x * width_y + width_y), 1.0, 0.0
    ).astype(BF16)
    hot_xt3 = jnp.concatenate([hot_xt] * 3, axis=1)
    well_col = as_column(well_v[...].astype(F32)).astype(jnp.int32)
    owner_col = as_column(owner_v[...].astype(F32)).astype(jnp.int32)
    well_id = owner_col * own_wells + well_col
    member = jnp.where(
        (lax.broadcasted_iota(jnp.int32, (slots, wells), 1) == well_id) & live, 1.0, 0.0
    )
    layer_lane = lax.broadcasted_iota(jnp.int32, (slots, depth), 1)
    index = jnp.zeros((slots, depth), F32)
    for l in range(depth):
        index = jnp.where(layer_lane == l, as_column(index_v[l : l + 1, :]), index)
    rate_col = as_column(rate_v[...])
    rate_spot = (
        lax.broadcasted_iota(jnp.int32, (own_wells, wells), 1)
        == lax.broadcasted_iota(jnp.int32, (own_wells, wells), 0) + me * own_wells
    )
    rate_row = jnp.sum(jnp.where(rate_spot, rate_col, 0.0), axis=0, keepdims=True)

    def gathered():
        at = jnp.zeros((slots, depth), F32)
        for l in range(depth):
            picked = jnp.dot(hot_x3, pieces(field[l]), preferred_element_type=F32)
            one = jnp.sum(jnp.where(in_y, picked, 0.0), axis=1, keepdims=True)
            at = jnp.where(layer_lane == l, one, at)
        return at

    def well_row(at):
        share = jnp.sum(index * at, axis=1, keepdims=True)
        return jnp.sum(share * member, axis=0, keepdims=True) + rate_row

    def well_copy(it, step):
        send, recv = ((well_send0, well_recv0), (well_send1, well_recv1))[it]
        return pltpu.make_async_remote_copy(
            src_ref=send,
            dst_ref=recv.at[step],
            send_sem=well_ssem.at[it, step],
            recv_sem=well_rsem.at[it, step],
            device_id=peer(step),
            device_id_type=MESH,
        )

    sides = (
        ("gx", me_x, -1, me_x > 0),
        ("gx", me_x, 1, me_x < n_gx - 1),
        ("gy", me_y, -1, me_y > 0),
        ("gy", me_y, 1, me_y < n_gy - 1),
    )

    def halo_copy(it, side):
        axis, mine, way, _ = sides[side]
        send, recv = (row_send, row_recv) if side < 2 else (col_send, col_recv)
        width = slice(0, 2 if it == 0 else 1)
        if side < 2:
            source_ref = send.at[it, side, width]
            target_ref = recv.at[it, 1 - side, width]
        else:
            source_ref = send.at[it, side - 2]
            target_ref = recv.at[it, 3 - side]
        return pltpu.make_async_remote_copy(
            src_ref=source_ref,
            dst_ref=target_ref,
            send_sem=halo_ssem.at[it, side],
            recv_sem=halo_rsem.at[it, side ^ 1],
            device_id={axis: mine + way},
            device_id_type=MESH,
        )

    def halo_landing(it, side):
        axis, mine, way, _ = sides[side]
        if side < 2:
            width = slice(0, 2 if it == 0 else 1)
            ref, other = row_recv.at[it, side, width], row_send.at[it, 1 - side, width]
        else:
            ref, other = col_recv.at[it, side - 2], col_send.at[it, 3 - side]
        return pltpu.make_async_remote_copy(
            src_ref=other,
            dst_ref=ref,
            send_sem=halo_ssem.at[it, side],
            recv_sem=halo_rsem.at[it, side],
            device_id={axis: mine + way},
            device_id_type=MESH,
        )

    lane128 = lax.broadcasted_iota(jnp.int32, (width_x, 128), 1)

    def packed_columns(arrays, lane):
        out = jnp.zeros((width_x, 128), F32)
        at = 0
        for ref in arrays:
            for l in range(depth):
                out = jnp.where(lane128 == at, ref[l, :, lane : lane + 1], out)
                at += 1
        return out

    def stage_halos(it):
        for l in range(depth):
            row_send[it, 0, 0, l : l + 1, :] = field[l, 0:1, :]
            row_send[it, 1, 0, l : l + 1, :] = field[l, width_x - 1 : width_x, :]
            if it == 0:
                row_send[it, 0, 1, l : l + 1, :] = kx[l, 0:1, :]
                row_send[it, 1, 1, l : l + 1, :] = kx[l, width_x - 1 : width_x, :]
        arrays = (field, ky) if it == 0 else (field,)
        col_send[it, 0] = packed_columns(arrays, 0)
        col_send[it, 1] = packed_columns(arrays, width_y - 1)
        for side in range(4):

            @pl.when(jnp.logical_not(sides[side][3]))
            def _():
                if side < 2:
                    row_recv[it, side] = jnp.zeros(row_recv.shape[2:], F32)
                else:
                    col_recv[it, side - 2] = jnp.zeros(col_recv.shape[2:], F32)

    def start_halos(it):
        for side in range(4):
            @pl.when(sides[side][3])
            def _():
                halo_copy(it, side).start()

    def wait_halos(it):
        for side in range(4):
            @pl.when(sides[side][3])
            def _():
                halo_landing(it, side).wait_recv()

    last_x = lax.broadcasted_iota(jnp.int32, (width_x, width_y), 0) == width_x - 1
    first_x = lax.broadcasted_iota(jnp.int32, (width_x, width_y), 0) == 0
    last_y = lax.broadcasted_iota(jnp.int32, (width_x, width_y), 1) == width_y - 1
    first_y = lax.broadcasted_iota(jnp.int32, (width_x, width_y), 1) == 0

    def next_x(value, row):
        return jnp.where(last_x, row, pltpu.roll(value, width_x - 1, 0))

    def next_y(value, col):
        return jnp.where(last_y, col, pltpu.roll(value, width_y - 1, 1))

    def face_coefficients():
        for l in range(depth):
            row = kx[l, 0:1, :]
            halo_mult_x[l : l + 1, :] = 0.5 * (row + row_recv[0, 0, 1, l : l + 1, :])
            mult = kx[l]
            kx[l] = 0.5 * (mult + next_x(mult, row_recv[0, 1, 1, l : l + 1, :]))
            mult = ky[l]
            ky[l] = 0.5 * (mult + next_y(mult, col_recv[0, 1, :, depth + l : depth + l + 1]))
        halo_mult_y[...] = 0.5 * (col_send[0, 0] + col_recv[0, 0])

    def lateral_sum(it):
        for l in range(depth):
            now = field[l]
            face_x, face_y = kx[l], ky[l]
            east = face_x * next_x(now, row_recv[it, 1, 0, l : l + 1, :])
            west_row = halo_mult_x[l : l + 1, :] * row_recv[it, 0, 0, l : l + 1, :]
            west = jnp.where(first_x, west_row, pltpu.roll(face_x * now, 1, 0))
            north = face_y * next_y(now, col_recv[it, 1, :, l : l + 1])
            south_col = halo_mult_y[:, depth + l : depth + l + 1] * col_recv[it, 0, :, l : l + 1]
            south = jnp.where(first_y, south_col, pltpu.roll(face_y * now, 1, 1))
            rhs[l] = src[l] + ((east + west) + (north + south))

    def layer_copy(ref, target, ssem, rsem, other):
        return pltpu.make_async_remote_copy(
            src_ref=ref,
            dst_ref=target,
            send_sem=ssem,
            recv_sem=rsem,
            device_id={"layer": other},
            device_id_type=MESH,
        )

    last = depth - 1
    coef_at = ((0, 0), (0, last), (last, 0))[: 1 if groups == 2 else 3]

    def coef_copy(which, sender, other):
        i, j = coef_at[which]
        return layer_copy(
            inv.at[i, j],
            coef_recv.at[sender, which],
            coef_ssem.at[other, which],
            coef_rsem.at[sender, which],
            other,
        )

    def coef_sent(which, sender, other):
        if which == 0:
            return other < sender
        if which == 1:
            return other < sender < groups - 1
        return 0 < sender < groups - 1

    def down_copy(it, sender, other):
        return layer_copy(
            down_send.at[it], down_recv.at[it, sender], down_ssem.at[it, other],
            down_rsem.at[it, sender], other,
        )

    def up_copy(it, sender, other):
        return layer_copy(
            up_send.at[it], up_recv.at[it, sender], up_ssem.at[it, other],
            up_rsem.at[it, sender], other,
        )

    def layer_sends(act, which):
        for g in range(groups):

            @pl.when(me_l == g)
            def _():
                for other in range(groups):
                    if other == g:
                        continue
                    if which == "coef":
                        for c in range(len(coef_at)):
                            if coef_sent(c, g, other):
                                getattr(coef_copy(c, g, other), act)()
                    else:
                        it = which
                        if g < groups - 1:
                            getattr(down_copy(it, g, other), act)()
                        if other < g:
                            getattr(up_copy(it, g, other), act)()

    def chunk_loop(body):
        def step(c, carry):
            body(pl.ds(pl.multiple_of(c * ROWS, ROWS), ROWS))
            return carry

        lax.fori_loop(0, width_x // ROWS, step, 0)

    def dot_layer(i, rows, terms):
        total = inv[i, 0, rows, :] * terms[0]
        for j in range(1, depth):
            total = total + inv[i, j, rows, :] * terms[j]
        return total

    def solve_faces(it):
        def body(rows):
            terms = [rhs[j, rows, :] for j in range(depth)]
            bottom = dot_layer(last, rows, terms)
            top = dot_layer(0, rows, terms)
            solved[last, rows, :] = bottom
            solved[0, rows, :] = top
            below = lower[rows, :]
            nothing = jnp.zeros_like(below)
            down_send[it, rows, :] = inv[last, 0, rows, :] * nothing + (
                (bottom + inv[last, last, rows, :] * below) - below
            )
            up_send[it, rows, :] = inv[0, last, rows, :] * nothing + top

        chunk_loop(body)

    def solve_rest():
        def body(rows):
            terms = [rhs[j, rows, :] for j in range(depth)]
            for i in range(1, depth - 1):
                solved[i, rows, :] = dot_layer(i, rows, terms)

        chunk_loop(body)

    def sweeps(it):
        for g in range(groups):

            @pl.when(me_l == g)
            def _():
                for k in range(groups):
                    if k == g:
                        continue
                    if k < groups - 1:
                        down_copy(it, k, k).wait_recv()
                    if k > g:
                        up_copy(it, k, k).wait_recv()
                    if it == 0:
                        for c in range(len(coef_at)):
                            if coef_sent(c, k, g):
                                coef_copy(c, k, k).wait_recv()

                def body(rows):
                    def coef(which, k):
                        i, j = coef_at[which]
                        return inv[i, j, rows, :] if k == g else coef_recv[k, which, rows, :]

                    above = [jnp.zeros((ROWS, width_y), F32)]
                    for k in range(groups - 1):
                        value = down_send[it, rows, :] if k == g else down_recv[it, k, rows, :]
                        if k > 0:
                            value = coef(2, k) * above[k] + value
                        above.append(value)
                    below = jnp.zeros((ROWS, width_y), F32)
                    for k in range(groups - 1, g, -1):
                        value = (up_recv[it, k, rows, :] + coef(0, k) * above[k]) - above[k]
                        if k < groups - 1:
                            value = coef(1, k) * below + value
                        below = value
                    upper[rows, :] = above[g]
                    lower[rows, :] = below

                chunk_loop(body)

    def update():
        def body(rows):
            above, below = upper[rows, :], lower[rows, :]
            for i in range(depth):
                field[i, rows, :] = (
                    solved[i, rows, :]
                    + inv[i, 0, rows, :] * above
                    + inv[i, last, rows, :] * below
                )

        chunk_loop(body)

    index_total = None
    for it in range(ITERS):
        if it == 0:
            loads[0].wait()
        at = gathered()
        if it == 0:
            index_row = jnp.sum(
                jnp.sum(index, axis=1, keepdims=True) * member, axis=0, keepdims=True
            )
            well_send0[...] = jnp.concatenate([well_row(at), index_row], axis=1)
            pl.semaphore_wait(barrier, tiles - 1 + groups - 1)
        else:
            well_send1[...] = well_row(at)
        for step in range(1, tiles):
            well_copy(it, step).start()
        if it == 0:
            loads[7].wait()
            loads[8].wait()
        stage_halos(it)
        start_halos(it)
        if it == 0:
            for load in loads[9:]:
                load.wait()
            layer_sends("start", "coef")
        wait_halos(it)
        if it == 0:
            face_coefficients()
        lateral_sum(it)
        total = (well_send0, well_send1)[it][...]
        for step in range(1, tiles):
            well_copy(it, step).wait_recv()
        for step in range(1, tiles):
            total = total + (well_recv0, well_recv1)[it][step]
        if it == 0:
            index_total = total[:, wells:] + 1.0
            total = total[:, :wells]
        bottom_hole = total / index_total
        hole = jnp.sum(member * bottom_hole, axis=1, keepdims=True)
        flow = jnp.where(live, index * (hole - at), 0.0)
        if it == ITERS - 1:
            for l in range(depth):
                flow_v[l : l + 1, :] = as_row(flow[:, l : l + 1])
            flow_store = pltpu.make_async_copy(flow_v, flow_out, store_sem.at[0])
            flow_store.start()
        for l in range(depth):
            spread = jnp.where(in_y, flow[:, l : l + 1], 0.0)
            rhs[l] = rhs[l] + jnp.dot(hot_xt3, pieces(spread), preferred_element_type=F32)
        solve_faces(it)
        layer_sends("start", it)
        solve_rest()
        sweeps(it)
        update()
    field_store = pltpu.make_async_copy(field, field_out, store_sem.at[1])
    field_store.start()
    for it in range(ITERS):
        for step in range(1, tiles):
            well_copy(it, step).wait_send()
        for side in range(4):

            @pl.when(sides[side][3])
            def _():
                halo_copy(it, side).wait_send()

        layer_sends("wait_send", it)
    layer_sends("wait_send", "coef")
    flow_store.wait()
    field_store.wait()


def shards(
    pressure,
    source,
    perm_x,
    perm_y,
    line_inverse,
    robin_below,
    tile_count,
    perf_owner,
    perf_well,
    perf_column,
    perf_index,
    well_rate,
):
    depth, width_x, width_y = pressure.shape
    groups, n_gx, n_gy = (lax.axis_size(a) for a in ("layer", "gx", "gy"))
    tiles = n_gx * n_gy
    slots = perf_well.shape[1]
    own_wells = well_rate.shape[1]
    wells = tiles * own_wells
    sheet = (width_x, width_y)
    coefs = 1 if groups == 2 else 3
    HBM = pl.BlockSpec(memory_space=pltpu.HBM)
    anywhere = pl.BlockSpec(memory_space=pl.ANY)
    dma = pltpu.SemaphoreType.DMA
    i32 = jnp.int32
    call = pl.pallas_call(
        functools.partial(kernel, (groups, n_gx, n_gy)),
        out_shape=(
            jax.ShapeDtypeStruct(pressure.shape, F32),
            jax.ShapeDtypeStruct((depth, slots), F32),
        ),
        in_specs=[HBM] * 12,
        out_specs=(anywhere, anywhere),
        scratch_shapes=[
            pltpu.VMEM(pressure.shape, F32),
            pltpu.VMEM(pressure.shape, F32),
            pltpu.VMEM(pressure.shape, F32),
            pltpu.VMEM(pressure.shape, F32),
            pltpu.VMEM((depth, depth) + sheet, F32),
            pltpu.VMEM(sheet, F32),
            pltpu.VMEM((1, 1), i32),
            pltpu.VMEM((1, slots), i32),
            pltpu.VMEM((1, slots), i32),
            pltpu.VMEM((1, slots), i32),
            pltpu.VMEM((depth, slots), F32),
            pltpu.VMEM((1, own_wells), F32),
            pltpu.VMEM(sheet, F32),
            pltpu.VMEM(pressure.shape, F32),
            pltpu.VMEM(pressure.shape, F32),
            pltpu.VMEM((depth, slots), F32),
            pltpu.VMEM((depth, width_y), F32),
            pltpu.VMEM((width_x, 128), F32),
            pltpu.VMEM((1, 2 * wells), F32),
            pltpu.VMEM((tiles, 1, 2 * wells), F32),
            pltpu.VMEM((1, wells), F32),
            pltpu.VMEM((tiles, 1, wells), F32),
            pltpu.VMEM((ITERS, 2, 2, depth, width_y), F32),
            pltpu.VMEM((ITERS, 2, 2, depth, width_y), F32),
            pltpu.VMEM((ITERS, 2, width_x, 128), F32),
            pltpu.VMEM((ITERS, 2, width_x, 128), F32),
            pltpu.VMEM((groups, coefs) + sheet, F32),
            pltpu.VMEM((ITERS,) + sheet, F32),
            pltpu.VMEM((ITERS, groups) + sheet, F32),
            pltpu.VMEM((ITERS,) + sheet, F32),
            pltpu.VMEM((ITERS, groups) + sheet, F32),
            dma((12,)),
            dma((2,)),
            dma((ITERS, tiles)),
            dma((ITERS, tiles)),
            dma((ITERS, 4)),
            dma((ITERS, 4)),
            dma((groups, coefs)),
            dma((groups, coefs)),
            dma((ITERS, groups)),
            dma((ITERS, groups)),
            dma((ITERS, groups)),
            dma((ITERS, groups)),
        ],
        compiler_params=pltpu.CompilerParams(collective_id=0, has_side_effects=True, vmem_limit_bytes=LIMIT),
        name="window",
    )
    operands = (
        pressure,
        source,
        perm_x,
        perm_y,
        line_inverse[0],
        robin_below[0],
        tile_count,
        perf_owner[:, :, 0],
        perf_well,
        perf_column,
        perf_index[0].T,
        well_rate,
    )
    field, flow = call(
        *[x if x.size == 1 else pltpu.with_memory_space_constraint(x, pltpu.HBM) for x in operands]
    )
    field, flow = pl.pallas_call(
        keep,
        out_shape=(
            jax.ShapeDtypeStruct(field.shape, F32),
            jax.ShapeDtypeStruct(flow.shape, F32),
        ),
        in_specs=[anywhere] * 2,
        out_specs=(HBM, HBM),
        scratch_shapes=[dma((2,))],
        compiler_params=pltpu.CompilerParams(vmem_limit_bytes=1 << 20),
        name="keep",
    )(field, flow)
    return field, flow.T[None]


def solution(mesh):
    placed = (
        P("layer", "gx", "gy"),
        P("layer", "gx", "gy"),
        P("layer", "gx", "gy"),
        P("layer", "gx", "gy"),
        P("layer", None, None, "gx", "gy"),
        P("layer", "gx", "gy"),
        P("layer", ("gx", "gy")),
        P("layer", ("gx", "gy"), None),
        P("layer", ("gx", "gy")),
        P("layer", ("gx", "gy")),
        P("layer", ("gx", "gy"), None),
        P("layer", ("gx", "gy")),
    )
    return jax.shard_map(
        shards,
        mesh=mesh,
        in_specs=placed,
        out_specs=(P("layer", "gx", "gy"), P("layer", ("gx", "gy"), None)),
        check_vma=False,
    )
```

```python
import functools

import jax
import jax.numpy as jnp
from jax import lax
from jax.experimental import pallas as pl
from jax.experimental.pallas import tpu as pltpu
from jax.sharding import PartitionSpec as P

ITERS = 2
LIMIT = 24 << 20
MESH = pl.DeviceIdType.MESH
F32 = jnp.float32
BF16 = jnp.bfloat16
ROWS = 8


def pieces(value):
    high = value.astype(BF16)
    rest = value - high.astype(F32)
    middle = rest.astype(BF16)
    low = (rest - middle.astype(F32)).astype(BF16)
    return jnp.concatenate([high, middle, low], axis=0)


def as_column(row):
    n = row.shape[1]
    eye = lax.broadcasted_iota(jnp.int32, (n, n), 0) == lax.broadcasted_iota(jnp.int32, (n, n), 1)
    return jnp.sum(jnp.where(eye, jnp.broadcast_to(row, (n, n)), 0.0), axis=1, keepdims=True)


def as_row(column):
    n = column.shape[0]
    eye = lax.broadcasted_iota(jnp.int32, (n, n), 0) == lax.broadcasted_iota(jnp.int32, (n, n), 1)
    return jnp.sum(jnp.where(eye, jnp.broadcast_to(column, (n, n)), 0.0), axis=0, keepdims=True)


def one_hots(column_row, width_x, width_y):
    slots = column_row.shape[1]
    column_col = as_column(column_row.astype(F32)).astype(jnp.int32)
    lane_x = lax.broadcasted_iota(jnp.int32, (slots, width_x), 1)
    in_x = (column_col >= lane_x * width_y) & (column_col < lane_x * width_y + width_y)
    x_of = jnp.sum(jnp.where(in_x, lane_x.astype(F32), 0.0), axis=1, keepdims=True).astype(jnp.int32)
    in_y = lax.broadcasted_iota(jnp.int32, (slots, width_y), 1) == column_col - x_of * width_y
    hot_x = jnp.where(in_x, 1.0, 0.0).astype(BF16)
    row_x = lax.broadcasted_iota(jnp.int32, (width_x, slots), 0)
    hot_xt = jnp.where(
        (column_row >= row_x * width_y) & (column_row < row_x * width_y + width_y), 1.0, 0.0
    ).astype(BF16)
    return in_y, jnp.concatenate([hot_x] * 3, axis=1), jnp.concatenate([hot_xt] * 3, axis=1)


def keep(field_in, flow_in, field_out, flow_out, sem):
    copies = [
        pltpu.make_async_copy(field_in, field_out, sem.at[0]),
        pltpu.make_async_copy(flow_in, flow_out, sem.at[1]),
    ]
    for copy in copies:
        copy.start()
    for copy in copies:
        copy.wait()


def kernel(
    dims,
    pressure,
    source,
    perm_x,
    perm_y,
    inverse,
    robin,
    count_in,
    owner_in,
    well_in,
    column_in,
    index_in,
    rate_in,
    field_out,
    flow_out,
    field,
    src,
    kx,
    ky,
    inv,
    lower,
    count_v,
    owner_v,
    well_v,
    column_v,
    index_v,
    rate_v,
    upper,
    rhs,
    solved,
    flow_v,
    halo_mult_x,
    halo_mult_y,
    well_send0,
    well_recv0,
    well_send1,
    well_recv1,
    row_send,
    row_recv,
    col_send,
    col_recv,
    coef_recv,
    down_send,
    down_recv,
    up_send,
    up_recv,
    own_down,
    spot_recv,
    delta_send,
    delta_recv,
    load_sem,
    store_sem,
    well_ssem,
    well_rsem,
    halo_ssem,
    halo_rsem,
    coef_ssem,
    coef_rsem,
    down_ssem,
    down_rsem,
    up_ssem,
    up_rsem,
    spot_ssem,
    spot_rsem,
    delta_ssem,
    delta_rsem,
):
    groups, n_gx, n_gy = dims
    tiles = n_gx * n_gy
    depth, width_x, width_y = field.shape
    slots = well_v.shape[1]
    own_wells = rate_v.shape[1]
    wells = tiles * own_wells
    me_l, me_x, me_y = lax.axis_index("layer"), lax.axis_index("gx"), lax.axis_index("gy")
    me = me_x * n_gy + me_y

    loads = [
        pltpu.make_async_copy(a, b, load_sem.at[i])
        for i, (a, b) in enumerate(
            [
                (pressure, field),
                (column_in, column_v),
                (well_in, well_v),
                (owner_in, owner_v),
                (index_in, index_v),
                (count_in, count_v),
                (rate_in, rate_v),
                (perm_x, kx),
                (perm_y, ky),
                (source, src),
                (robin, lower),
                (inverse, inv),
            ]
        )
    ]
    for load in loads:
        load.start()

    def peer(step):
        other = lax.rem(me + step, tiles)
        return {"gx": lax.div(other, n_gy), "gy": lax.rem(other, n_gy)}

    barrier = pltpu.get_barrier_semaphore()
    for step in range(1, tiles):
        pl.semaphore_signal(barrier, inc=1, device_id=peer(step), device_id_type=MESH)
    for step in range(1, groups):
        pl.semaphore_signal(
            barrier, inc=1, device_id={"layer": lax.rem(me_l + step, groups)}, device_id_type=MESH
        )

    for load in loads[1:7]:
        load.wait()
    live = lax.broadcasted_iota(jnp.int32, (slots, 1), 0) < count_v[...]
    in_y, hot_x3, hot_xt3 = one_hots(column_v[...], width_x, width_y)
    well_col = as_column(well_v[...].astype(F32)).astype(jnp.int32)
    owner_col = as_column(owner_v[...].astype(F32)).astype(jnp.int32)
    well_id = owner_col * own_wells + well_col
    member = jnp.where(
        (lax.broadcasted_iota(jnp.int32, (slots, wells), 1) == well_id) & live, 1.0, 0.0
    )
    layer_lane = lax.broadcasted_iota(jnp.int32, (slots, depth), 1)
    index = jnp.zeros((slots, depth), F32)
    for l in range(depth):
        index = jnp.where(layer_lane == l, as_column(index_v[l : l + 1, :]), index)
    rate_col = as_column(rate_v[...])
    rate_spot = (
        lax.broadcasted_iota(jnp.int32, (own_wells, wells), 1)
        == lax.broadcasted_iota(jnp.int32, (own_wells, wells), 0) + me * own_wells
    )
    rate_row = jnp.sum(jnp.where(rate_spot, rate_col, 0.0), axis=0, keepdims=True)

    def gathered(ref):
        at = jnp.zeros((slots, depth), F32)
        for l in range(depth):
            picked = jnp.dot(hot_x3, pieces(ref[l]), preferred_element_type=F32)
            one = jnp.sum(jnp.where(in_y, picked, 0.0), axis=1, keepdims=True)
            at = jnp.where(layer_lane == l, one, at)
        return at

    def well_row(at):
        share = jnp.sum(index * at, axis=1, keepdims=True)
        return jnp.sum(share * member, axis=0, keepdims=True) + rate_row

    def well_copy(it, step):
        send, recv = ((well_send0, well_recv0), (well_send1, well_recv1))[it]
        return pltpu.make_async_remote_copy(
            src_ref=send,
            dst_ref=recv.at[step],
            send_sem=well_ssem.at[it, step],
            recv_sem=well_rsem.at[it, step],
            device_id=peer(step),
            device_id_type=MESH,
        )

    sides = (
        ("gx", me_x, -1, me_x > 0),
        ("gx", me_x, 1, me_x < n_gx - 1),
        ("gy", me_y, -1, me_y > 0),
        ("gy", me_y, 1, me_y < n_gy - 1),
    )

    def halo_copy(it, side):
        axis, mine, way, _ = sides[side]
        send, recv = (row_send, row_recv) if side < 2 else (col_send, col_recv)
        width = slice(0, 2 if it == 0 else 1)
        if side < 2:
            source_ref = send.at[it, side, width]
            target_ref = recv.at[it, 1 - side, width]
        else:
            source_ref = send.at[it, side - 2]
            target_ref = recv.at[it, 3 - side]
        return pltpu.make_async_remote_copy(
            src_ref=source_ref,
            dst_ref=target_ref,
            send_sem=halo_ssem.at[it, side],
            recv_sem=halo_rsem.at[it, side ^ 1],
            device_id={axis: mine + way},
            device_id_type=MESH,
        )

    def halo_landing(it, side):
        axis, mine, way, _ = sides[side]
        if side < 2:
            width = slice(0, 2 if it == 0 else 1)
            ref, other = row_recv.at[it, side, width], row_send.at[it, 1 - side, width]
        else:
            ref, other = col_recv.at[it, side - 2], col_send.at[it, 3 - side]
        return pltpu.make_async_remote_copy(
            src_ref=other,
            dst_ref=ref,
            send_sem=halo_ssem.at[it, side],
            recv_sem=halo_rsem.at[it, side],
            device_id={axis: mine + way},
            device_id_type=MESH,
        )

    lane128 = lax.broadcasted_iota(jnp.int32, (width_x, 128), 1)

    def packed_columns(arrays, lane):
        out = jnp.zeros((width_x, 128), F32)
        at = 0
        for ref in arrays:
            for l in range(depth):
                out = jnp.where(lane128 == at, ref[l, :, lane : lane + 1], out)
                at += 1
        return out

    def stage_halos(it):
        for l in range(depth):
            row_send[it, 0, 0, l : l + 1, :] = field[l, 0:1, :]
            row_send[it, 1, 0, l : l + 1, :] = field[l, width_x - 1 : width_x, :]
            if it == 0:
                row_send[it, 0, 1, l : l + 1, :] = kx[l, 0:1, :]
                row_send[it, 1, 1, l : l + 1, :] = kx[l, width_x - 1 : width_x, :]
        arrays = (field, ky) if it == 0 else (field,)
        col_send[it, 0] = packed_columns(arrays, 0)
        col_send[it, 1] = packed_columns(arrays, width_y - 1)
        for side in range(4):

            @pl.when(jnp.logical_not(sides[side][3]))
            def _():
                if side < 2:
                    row_recv[it, side] = jnp.zeros(row_recv.shape[2:], F32)
                else:
                    col_recv[it, side - 2] = jnp.zeros(col_recv.shape[2:], F32)

    def start_halos(it):
        for side in range(4):
            @pl.when(sides[side][3])
            def _():
                halo_copy(it, side).start()

    def wait_halos(it):
        for side in range(4):
            @pl.when(sides[side][3])
            def _():
                halo_landing(it, side).wait_recv()

    last_x = lax.broadcasted_iota(jnp.int32, (width_x, width_y), 0) == width_x - 1
    first_x = lax.broadcasted_iota(jnp.int32, (width_x, width_y), 0) == 0
    last_y = lax.broadcasted_iota(jnp.int32, (width_x, width_y), 1) == width_y - 1
    first_y = lax.broadcasted_iota(jnp.int32, (width_x, width_y), 1) == 0

    def face_coefficients():
        for l in range(depth):
            mult = kx[l]
            kx[l] = 0.5 * (mult + pltpu.roll(mult, width_x - 1, 0))
            mult = ky[l]
            ky[l] = 0.5 * (mult + pltpu.roll(mult, width_y - 1, 1))

    def edge_coefficients():
        for l in range(depth):
            one = slice(l, l + 1)
            halo_mult_x[one, :] = 0.5 * (row_send[0, 0, 1, one, :] + row_recv[0, 0, 1, one, :])
            kx[l, width_x - 1 : width_x, :] = 0.5 * (
                row_send[0, 1, 1, one, :] + row_recv[0, 1, 1, one, :]
            )
            lane = slice(depth + l, depth + l + 1)
            ky[l, :, width_y - 1 : width_y] = 0.5 * (
                col_send[0, 1, :, lane] + col_recv[0, 1, :, lane]
            )
        halo_mult_y[...] = 0.5 * (col_send[0, 0] + col_recv[0, 0])

    def lateral_sum():
        for l in range(depth):
            now = field[l]
            face_x, face_y = kx[l], ky[l]
            east = jnp.where(last_x, 0.0, face_x * pltpu.roll(now, width_x - 1, 0))
            west = jnp.where(first_x, 0.0, pltpu.roll(face_x * now, 1, 0))
            north = jnp.where(last_y, 0.0, face_y * pltpu.roll(now, width_y - 1, 1))
            south = jnp.where(first_y, 0.0, pltpu.roll(face_y * now, 1, 1))
            rhs[l] = src[l] + ((east + west) + (north + south))

    def lateral_edges(it):
        end_x, end_y = slice(width_x - 1, width_x), slice(width_y - 1, width_y)
        for l in range(depth):
            one = slice(l, l + 1)
            lane = slice(depth + l, depth + l + 1)
            rhs[l, 0:1, :] += halo_mult_x[one, :] * row_recv[it, 0, 0, one, :]
            rhs[l, end_x, :] += kx[l, end_x, :] * row_recv[it, 1, 0, one, :]
            rhs[l, :, 0:1] += halo_mult_y[:, lane] * col_recv[it, 0, :, one]
            rhs[l, :, end_y] += ky[l, :, end_y] * col_recv[it, 1, :, one]

    def layer_copy(ref, target, ssem, rsem, other):
        return pltpu.make_async_remote_copy(
            src_ref=ref,
            dst_ref=target,
            send_sem=ssem,
            recv_sem=rsem,
            device_id={"layer": other},
            device_id_type=MESH,
        )

    last = depth - 1
    coef_at = ((0, 0), (0, last), (last, 0))[: 1 if groups == 2 else 3]

    def coef_copy(which, sender, other):
        i, j = coef_at[which]
        return layer_copy(
            inv.at[i, j],
            coef_recv.at[sender, which],
            coef_ssem.at[other, which],
            coef_rsem.at[sender, which],
            other,
        )

    def coef_sent(which, sender, other):
        if which == 0:
            return other < sender
        if which == 1:
            return other < sender < groups - 1
        return 0 < sender < groups - 1

    def spot_copy(step):
        return layer_copy(
            column_v, spot_recv.at[step], spot_ssem.at[step], spot_rsem.at[step],
            lax.rem(me_l + step, groups),
        )

    def delta_copy(it, step):
        return layer_copy(
            delta_send.at[it], delta_recv.at[it, step], delta_ssem.at[it, step],
            delta_rsem.at[it, step], lax.rem(me_l + step, groups),
        )

    def down_copy(it, sender, other):
        return layer_copy(
            down_send.at[it], down_recv.at[it, sender], down_ssem.at[it, other],
            down_rsem.at[it, sender], other,
        )

    def up_copy(it, sender, other):
        return layer_copy(
            up_send.at[it], up_recv.at[it, sender], up_ssem.at[it, other],
            up_rsem.at[it, sender], other,
        )

    def layer_sends(act, which):
        for g in range(groups):

            @pl.when(me_l == g)
            def _():
                for other in range(groups):
                    if other == g:
                        continue
                    if which == "coef":
                        for c in range(len(coef_at)):
                            if coef_sent(c, g, other):
                                getattr(coef_copy(c, g, other), act)()
                    else:
                        it = which
                        if g < groups - 1:
                            getattr(down_copy(it, g, other), act)()
                        if other < g:
                            getattr(up_copy(it, g, other), act)()

    def chunk_loop(body):
        def step(c, carry):
            body(pl.ds(pl.multiple_of(c * ROWS, ROWS), ROWS))
            return carry

        lax.fori_loop(0, width_x // ROWS, step, 0)

    def dot_layer(i, rows, terms):
        total = inv[i, 0, rows, :] * terms[0]
        for j in range(1, depth):
            total = total + inv[i, j, rows, :] * terms[j]
        return total

    def solve_faces(it):
        def body(rows):
            terms = [rhs[j, rows, :] for j in range(depth)]
            bottom = dot_layer(last, rows, terms)
            top = dot_layer(0, rows, terms)
            below = lower[rows, :]
            nothing = jnp.zeros_like(below)
            down_send[it, rows, :] = inv[last, 0, rows, :] * nothing + (
                (bottom + inv[last, last, rows, :] * below) - below
            )
            up_send[it, rows, :] = inv[0, last, rows, :] * nothing + top

        chunk_loop(body)

    def solve_all():
        def body(rows):
            terms = [rhs[j, rows, :] for j in range(depth)]
            for i in range(depth):
                value = dot_layer(i, rows, terms)
                solved[i, rows, :] = value
                if i == last:
                    below = lower[rows, :]
                    own_down[rows, :] = inv[last, 0, rows, :] * jnp.zeros_like(below) + (
                        (value + inv[last, last, rows, :] * below) - below
                    )

        chunk_loop(body)

    def sweeps(it):
        for g in range(groups):

            @pl.when(me_l == g)
            def _():
                for k in range(groups):
                    if k == g:
                        continue
                    if k < groups - 1:
                        down_copy(it, k, k).wait_recv()
                    if k > g:
                        up_copy(it, k, k).wait_recv()
                    if it == 0:
                        for c in range(len(coef_at)):
                            if coef_sent(c, k, g):
                                coef_copy(c, k, k).wait_recv()
                    step = (g - k) % groups
                    delta_copy(it, step).wait_recv()
                    other_y, _, other_xt3 = spots[step]
                    for row, wanted, ref in ((0, k < groups - 1, down_recv), (1, k > g, up_recv)):
                        if wanted:
                            spread = as_column(delta_recv[it, step, row : row + 1, :])
                            spread = pieces(jnp.where(other_y, spread, 0.0))
                            ref[it, k] = ref[it, k] + jnp.dot(
                                other_xt3, spread, preferred_element_type=F32
                            )

                def body(rows):
                    def coef(which, k):
                        i, j = coef_at[which]
                        return inv[i, j, rows, :] if k == g else coef_recv[k, which, rows, :]

                    above = [jnp.zeros((ROWS, width_y), F32)]
                    for k in range(groups - 1):
                        value = own_down[rows, :] if k == g else down_recv[it, k, rows, :]
                        if k > 0:
                            value = coef(2, k) * above[k] + value
                        above.append(value)
                    below = jnp.zeros((ROWS, width_y), F32)
                    for k in range(groups - 1, g, -1):
                        value = (up_recv[it, k, rows, :] + coef(0, k) * above[k]) - above[k]
                        if k < groups - 1:
                            value = coef(1, k) * below + value
                        below = value
                    upper[rows, :] = above[g]
                    lower[rows, :] = below

                chunk_loop(body)

    def update():
        def body(rows):
            above, below = upper[rows, :], lower[rows, :]
            for i in range(depth):
                field[i, rows, :] = (
                    solved[i, rows, :]
                    + inv[i, 0, rows, :] * above
                    + inv[i, last, rows, :] * below
                )

        chunk_loop(body)

    index_total = None
    spots = [None] * groups
    for it in range(ITERS):
        if it == 0:
            loads[0].wait()
        at = gathered(field)
        if it == 0:
            index_row = jnp.sum(
                jnp.sum(index, axis=1, keepdims=True) * member, axis=0, keepdims=True
            )
            well_send0[...] = jnp.concatenate([well_row(at), index_row], axis=1)
            loads[7].wait()
            loads[8].wait()
            stage_halos(it)
            pl.semaphore_wait(barrier, tiles - 1 + groups - 1)
        else:
            well_send1[...] = well_row(at)
        for step in range(1, tiles):
            well_copy(it, step).start()
        if it > 0:
            stage_halos(it)
        start_halos(it)
        if it == 0:
            for step in range(1, groups):
                spot_copy(step).start()
            for load in loads[9:]:
                load.wait()
            layer_sends("start", "coef")
        if it == 0:
            face_coefficients()
        lateral_sum()
        wait_halos(it)
        if it == 0:
            edge_coefficients()
        lateral_edges(it)
        solve_faces(it)
        layer_sends("start", it)
        if it == 0:
            for step in range(1, groups):
                spot_copy(step).wait_recv()
                spots[step] = one_hots(spot_recv[step], width_x, width_y)
            face_last, face_first = gathered(inv.at[last]), gathered(inv.at[0])
        total = (well_send0, well_send1)[it][...]
        for step in range(1, tiles):
            well_copy(it, step).wait_recv()
        for step in range(1, tiles):
            total = total + (well_recv0, well_recv1)[it][step]
        if it == 0:
            index_total = total[:, wells:] + 1.0
            total = total[:, :wells]
        bottom_hole = total / index_total
        hole = jnp.sum(member * bottom_hole, axis=1, keepdims=True)
        flow = jnp.where(live, index * (hole - at), 0.0)
        for row, face in enumerate((face_last, face_first)):
            delta_send[it, row : row + 1, :] = as_row(
                jnp.sum(face * flow, axis=1, keepdims=True)
            )
        for step in range(1, groups):
            delta_copy(it, step).start()
        if it == ITERS - 1:
            for l in range(depth):
                flow_v[l : l + 1, :] = as_row(flow[:, l : l + 1])
            flow_store = pltpu.make_async_copy(flow_v, flow_out, store_sem.at[0])
            flow_store.start()
        for l in range(depth):
            spread = jnp.where(in_y, flow[:, l : l + 1], 0.0)
            rhs[l] = rhs[l] + jnp.dot(hot_xt3, pieces(spread), preferred_element_type=F32)
        solve_all()
        sweeps(it)
        update()
    field_store = pltpu.make_async_copy(field, field_out, store_sem.at[1])
    field_store.start()
    for it in range(ITERS):
        for step in range(1, tiles):
            well_copy(it, step).wait_send()
        for side in range(4):

            @pl.when(sides[side][3])
            def _():
                halo_copy(it, side).wait_send()

        layer_sends("wait_send", it)
        for step in range(1, groups):
            delta_copy(it, step).wait_send()
    for step in range(1, groups):
        spot_copy(step).wait_send()
    layer_sends("wait_send", "coef")
    flow_store.wait()
    field_store.wait()


def shards(
    pressure,
    source,
    perm_x,
    perm_y,
    line_inverse,
    robin_below,
    tile_count,
    perf_owner,
    perf_well,
    perf_column,
    perf_index,
    well_rate,
):
    depth, width_x, width_y = pressure.shape
    groups, n_gx, n_gy = (lax.axis_size(a) for a in ("layer", "gx", "gy"))
    tiles = n_gx * n_gy
    slots = perf_well.shape[1]
    own_wells = well_rate.shape[1]
    wells = tiles * own_wells
    sheet = (width_x, width_y)
    coefs = 1 if groups == 2 else 3
    HBM = pl.BlockSpec(memory_space=pltpu.HBM)
    anywhere = pl.BlockSpec(memory_space=pl.ANY)
    dma = pltpu.SemaphoreType.DMA
    i32 = jnp.int32
    call = pl.pallas_call(
        functools.partial(kernel, (groups, n_gx, n_gy)),
        out_shape=(
            jax.ShapeDtypeStruct(pressure.shape, F32),
            jax.ShapeDtypeStruct((depth, slots), F32),
        ),
        in_specs=[HBM] * 12,
        out_specs=(anywhere, anywhere),
        scratch_shapes=[
            pltpu.VMEM(pressure.shape, F32),
            pltpu.VMEM(pressure.shape, F32),
            pltpu.VMEM(pressure.shape, F32),
            pltpu.VMEM(pressure.shape, F32),
            pltpu.VMEM((depth, depth) + sheet, F32),
            pltpu.VMEM(sheet, F32),
            pltpu.VMEM((1, 1), i32),
            pltpu.VMEM((1, slots), i32),
            pltpu.VMEM((1, slots), i32),
            pltpu.VMEM((1, slots), i32),
            pltpu.VMEM((depth, slots), F32),
            pltpu.VMEM((1, own_wells), F32),
            pltpu.VMEM(sheet, F32),
            pltpu.VMEM(pressure.shape, F32),
            pltpu.VMEM(pressure.shape, F32),
            pltpu.VMEM((depth, slots), F32),
            pltpu.VMEM((depth, width_y), F32),
            pltpu.VMEM((width_x, 128), F32),
            pltpu.VMEM((1, 2 * wells), F32),
            pltpu.VMEM((tiles, 1, 2 * wells), F32),
            pltpu.VMEM((1, wells), F32),
            pltpu.VMEM((tiles, 1, wells), F32),
            pltpu.VMEM((ITERS, 2, 2, depth, width_y), F32),
            pltpu.VMEM((ITERS, 2, 2, depth, width_y), F32),
            pltpu.VMEM((ITERS, 2, width_x, 128), F32),
            pltpu.VMEM((ITERS, 2, width_x, 128), F32),
            pltpu.VMEM((groups, coefs) + sheet, F32),
            pltpu.VMEM((ITERS,) + sheet, F32),
            pltpu.VMEM((ITERS, groups) + sheet, F32),
            pltpu.VMEM((ITERS,) + sheet, F32),
            pltpu.VMEM((ITERS, groups) + sheet, F32),
            pltpu.VMEM(sheet, F32),
            pltpu.VMEM((groups, 1, slots), i32),
            pltpu.VMEM((ITERS, 2, slots), F32),
            pltpu.VMEM((ITERS, groups, 2, slots), F32),
            dma((12,)),
            dma((2,)),
            dma((ITERS, tiles)),
            dma((ITERS, tiles)),
            dma((ITERS, 4)),
            dma((ITERS, 4)),
            dma((groups, coefs)),
            dma((groups, coefs)),
            dma((ITERS, groups)),
            dma((ITERS, groups)),
            dma((ITERS, groups)),
            dma((ITERS, groups)),
            dma((groups,)),
            dma((groups,)),
            dma((ITERS, groups)),
            dma((ITERS, groups)),
        ],
        compiler_params=pltpu.CompilerParams(collective_id=0, has_side_effects=True, vmem_limit_bytes=LIMIT),
        name="window",
    )
    operands = (
        pressure,
        source,
        perm_x,
        perm_y,
        line_inverse[0],
        robin_below[0],
        tile_count,
        perf_owner[:, :, 0],
        perf_well,
        perf_column,
        perf_index[0].T,
        well_rate,
    )
    field, flow = call(
        *[x if x.size == 1 else pltpu.with_memory_space_constraint(x, pltpu.HBM) for x in operands]
    )
    field, flow = pl.pallas_call(
        keep,
        out_shape=(
            jax.ShapeDtypeStruct(field.shape, F32),
            jax.ShapeDtypeStruct(flow.shape, F32),
        ),
        in_specs=[anywhere] * 2,
        out_specs=(HBM, HBM),
        scratch_shapes=[dma((2,))],
        compiler_params=pltpu.CompilerParams(vmem_limit_bytes=1 << 20),
        name="keep",
    )(field, flow)
    return field, flow.T[None]


def solution(mesh):
    placed = (
        P("layer", "gx", "gy"),
        P("layer", "gx", "gy"),
        P("layer", "gx", "gy"),
        P("layer", "gx", "gy"),
        P("layer", None, None, "gx", "gy"),
        P("layer", "gx", "gy"),
        P("layer", ("gx", "gy")),
        P("layer", ("gx", "gy"), None),
        P("layer", ("gx", "gy")),
        P("layer", ("gx", "gy")),
        P("layer", ("gx", "gy"), None),
        P("layer", ("gx", "gy")),
    )
    return jax.shard_map(
        shards,
        mesh=mesh,
        in_specs=placed,
        out_specs=(P("layer", "gx", "gy"), P("layer", ("gx", "gy"), None)),
        check_vma=False,
    )
```
